32 devices in a mesh: tok: 8 (over z, y), head: 4 (over x, core).
Axes of the slice: x: 2, y: 2, z: 4, core: 2. Of those that a mesh axis runs over, the one named last changes fastest.
Arguments:
- queries: bfloat16 [8192, 4096], P(('tok', 'head')), may hold values from -64 to 64
- keys: bfloat16 [8192, 4096], P(('tok', 'head')), may hold values from -6 to 6
- values: bfloat16 [8192, 4096], P(('tok', 'head')), may hold values from -6 to 6
- token_rates: bfloat16 [8192, 8], P(('tok', 'head')), may hold values from 0.099609375 to 1
- gate_start: bfloat16 [8, 512, 1024], P('head'), may hold values from -0.25 to 0.25
- up_start: bfloat16 [8, 512, 1024], P('head'), may hold values from -0.25 to 0.25
- down_start: bfloat16 [8, 1024, 512], P('head'), may hold values from -0.1875 to 0.1875
- norm_gain: float32 [4096], replicated, may hold values from 0.25 to 1.75
- bounds: int32 [4], replicated, may hold values from 896 to 1152
Outputs:
- layer_out: bfloat16 [8192, 4096], P(('tok', 'head'))
The draws below stay inside these ranges and needn't reach their ends.
Inputs may be any that keep to these rules, and one draw needn't show every extreme that they name: The first span of segment s is its positions below bounds[s].
All inputs are finite; a program needn't handle non-finite values.
Results may differ from the reference program's by a relative error of at most 0.02.
Values may be sent and summed in bfloat16 or wider, within the bound.
A program may use at most 192 MiB of HBM per device.

```python
import math
import jax
import jax.numpy as jnp
from jax import lax

FDIM = 512
HID = 1024
AHD = 128
WINDOW = 512
NS_ITERS = 3
FHEADS = 8
F = 4096
LEN = 2048
TOKENS = 8192
SEQS = 4
BOUND_LO = 896
BOUND_HI = 1152


def paired_fields(key):
    base_q = jnp.clip(jax.random.normal(jax.random.fold_in(key, 11), (TOKENS, F), jnp.float32), -6.0, 6.0)
    base_k = jnp.clip(jax.random.normal(jax.random.fold_in(key, 12), (TOKENS, F), jnp.float32), -6.0, 6.0)
    return (base_q, base_k)


def draw_queries(key, part):
    return paired_fields(key)[0].astype(jnp.bfloat16)


def draw_keys(key, part):
    return paired_fields(key)[1].astype(jnp.bfloat16)


def plant(drawn, own_key, low, top_value):
    longest = drawn.shape.index(max(drawn.shape))
    spots = []
    for shift in (0, 1):
        where = [jax.random.randint(jax.random.fold_in(own_key, axis), (), 0, length) for axis, length in enumerate(drawn.shape)]
        where[longest] = (where[longest] + shift) % drawn.shape[longest]
        spots.append(tuple(where))
    return drawn.at[spots[0]].set(low).at[spots[1]].set(top_value)


def steps_of(key, extent, pieces, least, high):
    def one(position, blocks):
        draws = jax.random.uniform(jax.random.fold_in(jax.random.fold_in(key, 6), position), (blocks,), jnp.float32, least / len(pieces), high / len(pieces))
        return jnp.repeat(jnp.exp(draws), extent[position] // blocks).reshape((-1,) + (1,) * (len(extent) - position - 1))

    level = one(*pieces[0])
    for cut in pieces[1:]:
        level = level * one(*cut)
    return level


def normal_values(own_key, shape, spread, most, split=(), kind=jnp.bfloat16):
    array = jax.random.normal(own_key, shape, jnp.float32) * spread
    if len(split) > 0:
        array = steps_of(own_key, shape, split, -0.22, 0.18) * array
    return jnp.clip(array, min=-most, max=most).astype(kind)


def setup_inputs(seed: int = 0) -> dict:
    seeds = jax.random.split(jax.random.key(seed), 10)
    return {
        "queries": draw_queries(jax.random.fold_in(seeds[9], 71), 0),
        "keys": draw_keys(jax.random.fold_in(seeds[9], 71), 0),
        "values": normal_values(seeds[2], (TOKENS, F), 1.0, 6.0, ((0, 32),)),
        "token_rates": jnp.clip(jnp.exp(math.log(1.0) - 2.306499 * jax.random.uniform(seeds[3], (TOKENS, FHEADS), jnp.float32) ** steps_of(seeds[3], (TOKENS, FHEADS), ((0, 32),), -0.2, 0.2)), 0.099609375, 1.0).astype(jnp.bfloat16),
        "gate_start": normal_values(seeds[4], (FHEADS, FDIM, HID), FDIM ** -0.5, 0.25, ((0, 4),)),
        "up_start": normal_values(seeds[5], (FHEADS, FDIM, HID), FDIM ** -0.5, 0.25, ((0, 4),)),
        "down_start": normal_values(seeds[6], (FHEADS, HID, FDIM), HID ** -0.5, 0.1875, ((0, 4),)),
        "norm_gain": jnp.clip(1.0 + 0.15 * jax.random.normal(seeds[7], (F,), jnp.float32), 0.25, 1.75),
        "bounds": plant(jax.random.randint(seeds[8], (SEQS,), BOUND_LO, BOUND_HI + 1), jax.random.fold_in(seeds[8], 1), BOUND_LO, BOUND_HI).astype(jnp.int32),
    }


linear_coef = 3.4445
cubic_coef = -4.775
quintic_coef = 2.0315
update_step = 1.0
rms_epsilon = 1e-05
norm_epsilon = 1e-06

def silu_slope(pre_act):
    logistic = jax.nn.sigmoid(pre_act)
    return logistic * (1.0 + pre_act * (1.0 - logistic))

def orthogonal(gradient):
    frob_norm = jnp.sqrt(jnp.sum(gradient * gradient) + norm_epsilon)
    iterate = (gradient / frob_norm).astype(jnp.bfloat16)
    for sweep_index in range(NS_ITERS):
        gram_matrix = jnp.dot(iterate, iterate.T, preferred_element_type=jnp.float32).astype(jnp.bfloat16)
        gram_square = jnp.dot(gram_matrix, gram_matrix, preferred_element_type=jnp.float32)
        poly_mix = (cubic_coef * gram_matrix.astype(jnp.float32) + quintic_coef * gram_square).astype(jnp.bfloat16)
        iterate = (linear_coef * iterate.astype(jnp.float32) + jnp.dot(poly_mix, iterate, preferred_element_type=jnp.float32)).astype(jnp.bfloat16)
    return iterate.astype(jnp.float32)

def renorm(updated, w_start):
    start_wide = w_start.astype(jnp.float32)
    target = jnp.sqrt(lax.optimization_barrier(jnp.sum(start_wide * start_wide, axis=0)) + norm_epsilon)
    actual = jnp.sqrt(lax.optimization_barrier(jnp.sum(updated * updated, axis=0)) + norm_epsilon)
    return (updated * (target / actual)).astype(jnp.bfloat16)

def swiglu_apply(in_rows, w_gate, w_up, w_down):
    pre_gate = jnp.dot(in_rows, w_gate, preferred_element_type=jnp.float32)
    pre_up = jnp.dot(in_rows, w_up, preferred_element_type=jnp.float32)
    hidden = (jax.nn.silu(pre_gate) * pre_up).astype(jnp.bfloat16)
    return jnp.dot(hidden, w_down, preferred_element_type=jnp.float32)

def fast_item(q_item, k_item, v_item, rate_row, span_bound, w_gate, w_up, w_down, gain_head):
    length = q_item.shape[0]
    split_low = length // 2 - length // 16
    split_high = length // 2 + length // 16
    in_span = jnp.arange(split_high) < span_bound
    k_rows = k_item[:split_high]
    pre_gate = jnp.dot(k_rows, w_gate, preferred_element_type=jnp.float32)
    pre_up = jnp.dot(k_rows, w_up, preferred_element_type=jnp.float32)
    active = jax.nn.silu(pre_gate)
    hidden = (active * pre_up).astype(jnp.bfloat16)
    weighted = rate_row[:split_high].astype(jnp.float32)[:, None] * v_item[:split_high].astype(jnp.float32)
    target = jnp.where(in_span[:, None], weighted, 0.0).astype(jnp.bfloat16)
    grad_down = jnp.dot(hidden.T, target, preferred_element_type=jnp.float32)
    back_grad = jnp.dot(target, w_down.T, preferred_element_type=jnp.float32)
    d_gate = (back_grad * pre_up * silu_slope(pre_gate)).astype(jnp.bfloat16)
    d_up = (back_grad * active).astype(jnp.bfloat16)
    grad_gate = jnp.dot(k_rows.T, d_gate, preferred_element_type=jnp.float32)
    grad_up = jnp.dot(k_rows.T, d_up, preferred_element_type=jnp.float32)
    new_gate = renorm(w_gate.astype(jnp.float32) + update_step * orthogonal(grad_gate), w_gate)
    new_up = renorm(w_up.astype(jnp.float32) + update_step * orthogonal(grad_up), w_up)
    new_down = renorm(w_down.astype(jnp.float32) + update_step * orthogonal(grad_down.T).T, w_down)
    before_out = swiglu_apply(q_item[:split_high], w_gate, w_up, w_down)
    after_out = swiglu_apply(q_item[split_low:], new_gate, new_up, new_down)
    middle = jnp.where((jnp.arange(split_low, split_high) < span_bound)[:, None], before_out[split_low:], after_out[:split_high - split_low])
    combined = jnp.concatenate([before_out[:split_low], middle, after_out[split_high - split_low:]], axis=0)
    root_mean = jnp.sqrt(lax.optimization_barrier(jnp.mean(combined * combined, axis=-1, keepdims=True)) + rms_epsilon)
    return (combined / root_mean * gain_head.astype(jnp.float32)).astype(jnp.bfloat16)

def attend_stream(queries, keys, values):
    block_len = min(LEN, 512)
    block_count = TOKENS // block_len
    head_count = F // AHD
    padding = jnp.zeros((WINDOW, F), keys.dtype)
    key_padded = jnp.concatenate([padding, keys], axis=0)
    value_padded = jnp.concatenate([padding, values], axis=0)

    def one_block(block_index):
        start = (block_index * block_len).astype(jnp.int32)
        q_rows = lax.dynamic_slice_in_dim(queries, start, block_len, 0)
        k_rows = lax.dynamic_slice_in_dim(key_padded, start, block_len + WINDOW, 0)
        v_rows = lax.dynamic_slice_in_dim(value_padded, start, block_len + WINDOW, 0)
        q_heads = q_rows.astype(jnp.float32).reshape(block_len, head_count, AHD)
        k_heads = k_rows.astype(jnp.float32).reshape(block_len + WINDOW, head_count, AHD)
        v_heads = v_rows.astype(jnp.float32).reshape(block_len + WINDOW, head_count, AHD)
        scores = jnp.einsum('qhd,khd->hqk', q_heads, k_heads) / math.sqrt(AHD)
        query_place = start + jnp.arange(block_len).astype(jnp.int32)
        key_place = start - WINDOW + jnp.arange(block_len + WINDOW).astype(jnp.int32)
        pos_gap = query_place[:, None] - key_place[None, :]
        allowed = ((pos_gap >= 0) & (pos_gap < WINDOW) & (key_place[None, :] >= 0))[None]
        masked = jnp.where(allowed, scores, -jnp.inf)
        row_max = lax.optimization_barrier(jnp.max(masked, axis=-1, keepdims=True))
        weights = jnp.where(allowed, jnp.exp(masked - row_max), 0.0)
        row_total = lax.optimization_barrier(jnp.sum(weights, axis=-1))
        mixed_out = jnp.einsum('hqk,khd->qhd', weights.astype(jnp.bfloat16).astype(jnp.float32), v_heads)
        return (mixed_out / row_total.T[:, :, None]).reshape(block_len, F).astype(jnp.bfloat16)
    return lax.map(one_block, jnp.arange(block_count).astype(jnp.int32)).reshape(TOKENS, F)

def reference(queries, keys, values, token_rates, gate_start, up_start, down_start, norm_gain, bounds):
    attn = attend_stream(queries, keys, values)

    def split_heads(block):
        return block.reshape(SEQS, LEN, FHEADS, FDIM).transpose(0, 2, 1, 3)
    rate_items = token_rates.reshape(SEQS, LEN, FHEADS).transpose(0, 2, 1)
    gain_items = norm_gain.reshape(FHEADS, FDIM)

    def per_sequence(seq_args):
        span_bound = seq_args[4]

        def per_head(head_args):
            return fast_item(head_args[0], head_args[1], head_args[2], head_args[3], span_bound, head_args[4], head_args[5], head_args[6], head_args[7])
        return lax.map(per_head, (seq_args[0], seq_args[1], seq_args[2], seq_args[3], gate_start, up_start, down_start, gain_items))
    fast_items = lax.map(per_sequence, (split_heads(queries), split_heads(keys), split_heads(values), rate_items, bounds))
    fast_rows = fast_items.transpose(0, 2, 1, 3).reshape(TOKENS, F)
    return (attn.astype(jnp.float32) + fast_rows.astype(jnp.float32)).astype(jnp.bfloat16)
```

```python
import functools
import math
from types import SimpleNamespace

import jax
import jax.numpy as jnp
from jax import lax
from jax.experimental import pallas as pl
from jax.experimental.pallas import tpu as pltpu
from jax.sharding import PartitionSpec as P

AHD = 128
WINDOW = 512
NS_ITERS = 3
CHUNK = 256

linear_coef = 3.4445
cubic_coef = -4.775
quintic_coef = 2.0315
rms_epsilon = 1e-05
norm_epsilon = 1e-06
MESH = pl.DeviceIdType.MESH
F32 = jnp.float32
BF16 = jnp.bfloat16


def mm(a, b, ca=1, cb=0):
    return lax.dot_general(a, b, (((ca,), (cb,)), ((), ())), preferred_element_type=F32)


def logistic(x):
    return 0.5 * jnp.tanh(0.5 * x) + 0.5


def loop(count, fn):
    def step(i, carry):
        fn(i)
        return carry

    lax.fori_loop(0, count, step, 0)


def at(start, size, multiple):
    return pl.ds(pl.multiple_of(start, multiple), size)


def transpose_down(c):
    def step(i):
        cols = at(i * CHUNK, CHUNK, CHUNK)
        c.wdt[:, cols] = c.wd[cols, :].T

    loop(c.hid_width // CHUNK, step)


def make_targets(c):
    per_block = c.rows // 128

    def step(i):
        rates = c.rates[i // per_block, 0:1, at((i % per_block) * 128, 128, 128)]
        rate_col = jnp.broadcast_to(rates, (128, 128)).T[:, 0:1]
        values = c.v[at(WINDOW + i * 128, 128, 128), :].astype(F32)
        place = i * 128 + lax.broadcasted_iota(jnp.int32, (128, c.width), 0)
        target = jnp.where(place < c.bound, rate_col * values, 0.0)
        c.target[at(i * 128, 128, 128), :] = target.astype(BF16)
        c.target_t[:, at(i * 128, 128, 128)] = target.T.astype(BF16)
        c.k_t[:, at(i * 128, 128, 128)] = c.k[at(WINDOW + i * 128, 128, 128), :].T

    loop(c.high // 128, step)


def backward(c):
    tile = c.tile
    chunks = c.hid_width // CHUNK

    def step(i):
        rows = at((i // chunks) * tile, tile, 128)
        cols = at((i % chunks) * CHUNK, CHUNK, CHUNK)
        k_rows = c.k[at(WINDOW + (i // chunks) * tile, tile, 128), :]
        gate = mm(k_rows, c.wg[:, cols])
        up = mm(k_rows, c.wu[:, cols])
        back = mm(c.target[rows, :], c.wdt[:, cols])
        sig = logistic(gate)
        act = gate * sig
        c.hid[rows, cols] = (act * up).astype(BF16)
        c.d_gate[rows, cols] = (back * up * (sig + act * (1.0 - sig))).astype(BF16)
        c.d_up[rows, cols] = (back * act).astype(BF16)

    loop((c.high // tile) * chunks, step)


def gradients(c):
    def step(i):
        cols = at(i * CHUNK, CHUNK, CHUNK)
        c.grad[0, :, cols] = mm(c.k_t[...], c.d_gate[:, cols])
        c.grad[1, :, cols] = mm(c.k_t[...], c.d_up[:, cols])
        c.grad[2, :, cols] = mm(c.target_t[...], c.hid[:, cols])

    loop(c.hid_width // CHUNK, step)

    def scale(m):
        grad = c.grad[m]
        frob = lax.rsqrt(jnp.sum(grad * grad, keepdims=True) + norm_epsilon)
        c.x[m] = (grad * frob).astype(BF16)

    loop(3, scale)


def newton(c):
    def sweep(_):
        for m in range(3):
            x = c.x[m]
            c.a[m] = mm(x, x, 1, 1).astype(BF16)
        for m in range(3):
            a = c.a[m]
            c.p[m] = (cubic_coef * a.astype(F32) + quintic_coef * mm(a, a)).astype(BF16)
        for m in range(3):
            x = c.x[m]
            c.y[m] = (linear_coef * x.astype(F32) + mm(c.p[m], x)).astype(BF16)
        c.x[...] = c.y[...]

    loop(NS_ITERS, sweep)


def renorm(c):
    def by_column(i):
        cols = at(i * CHUNK, CHUNK, CHUNK)
        for m, ref in ((0, c.wg), (1, c.wu)):
            w = ref[:, cols].astype(F32)
            u = w + c.x[m, :, cols].astype(F32)
            want = jnp.sqrt(jnp.sum(w * w, axis=0, keepdims=True) + norm_epsilon)
            have = jnp.sqrt(jnp.sum(u * u, axis=0, keepdims=True) + norm_epsilon)
            c.x[m, :, cols] = (u * (want / have)).astype(BF16)

    loop(c.hid_width // CHUNK, by_column)

    def by_row(i):
        rows = at(i * 128, 128, 128)
        w = c.wdt[rows, :].astype(F32)
        u = w + c.x[2, rows, :].astype(F32)
        want = jnp.sqrt(jnp.sum(w * w, axis=1, keepdims=True) + norm_epsilon)
        have = jnp.sqrt(jnp.sum(u * u, axis=1, keepdims=True) + norm_epsilon)
        c.x[2, rows, :] = (u * (want / have)).astype(BF16)

    loop(c.width // 128, by_row)


def attention(c):
    tile = WINDOW // 2
    power = math.log2(math.e) / math.sqrt(AHD)

    def step(t):
        rows = at(t * tile, tile, tile)
        span = at(t * tile, WINDOW + tile, tile)
        below = lax.broadcasted_iota(jnp.int32, (tile, tile), 1) <= lax.broadcasted_iota(
            jnp.int32, (tile, tile), 0
        )
        far_bias = jnp.where(c.first_segment * (2 - t) > 0, F32(-1e30), F32(0.0))
        mid_bias = jnp.where(c.first_segment * (1 - t) > 0, F32(-1e30), F32(0.0))
        for head in range(c.width // AHD):
            feats = slice(head * AHD, (head + 1) * AHD)
            scores = mm(c.q[rows, feats], c.k[span, feats], 1, 1)
            edge = jnp.where(below, scores[:, 2 * tile :], scores[:, :tile] + far_bias)
            mid = scores[:, tile : 2 * tile] + mid_bias
            top = jnp.max(jnp.maximum(edge, mid), axis=1, keepdims=True)
            edge = jnp.exp2((edge - top) * power)
            mid = jnp.exp2((mid - top) * power)
            total = jnp.sum(edge + mid, axis=1, keepdims=True)
            weights = jnp.concatenate(
                [
                    jnp.where(below, 0.0, edge).astype(BF16),
                    mid.astype(BF16),
                    jnp.where(below, edge, 0.0).astype(BF16),
                ],
                axis=1,
            )
            mixed = mm(weights, c.v[span, feats])
            c.out[rows, feats] = (mixed / total).astype(BF16)

    loop(c.length // tile, step)


def finish(c, start, raw):
    rows = at(start, raw.shape[0], 128)
    scale = lax.rsqrt(jnp.mean(raw * raw, axis=1, keepdims=True) + rms_epsilon)
    fast = (raw * scale * c.gain).astype(BF16)
    c.out[rows, :] = (c.out[rows, :].astype(F32) + fast.astype(F32)).astype(BF16)


def hidden_rows(c, start, gate_of, up_of):
    q_rows = c.q[at(start, c.tile, 128), :]

    def step(i):
        cols = at(i * CHUNK, CHUNK, CHUNK)
        gate = mm(q_rows, gate_of(cols))
        up = mm(q_rows, up_of(cols))
        c.apply_hid[:, cols] = (gate * logistic(gate) * up).astype(BF16)

    loop(c.hid_width // CHUNK, step)


def apply_old(c, sent=lambda done: None):
    tile = c.tile
    count = c.high // tile

    def body(i):
        hidden_rows(c, i * tile, lambda cols: c.wg[:, cols], lambda cols: c.wu[:, cols])
        c.raw[...] = mm(c.apply_hid[...], c.wd[...])

    def step(i):
        body(i)
        finish(c, i * tile, c.raw[...])

    loop(count - 1, step)
    body(count - 1)
    low_rows = c.low - (count - 1) * tile
    finish(c, (count - 1) * tile, c.raw[:low_rows, :])
    c.mid[...] = c.raw[low_rows:, :]


def apply_new(c, i):
    tile = c.tile
    both = c.high - c.low
    start = c.low + i * tile
    hidden_rows(c, start, lambda cols: c.x[0, :, cols], lambda cols: c.x[1, :, cols])
    raw = mm(c.apply_hid[...], c.x[2], 1, 1)
    if i == 0:
        place = c.low + lax.broadcasted_iota(jnp.int32, (both, c.width), 0)
        finish(c, c.low, jnp.where(place < c.bound, c.mid[...], raw[:both]))
        finish(c, c.low + both, raw[both:])
    else:
        finish(c, start, raw)


def scratch_of(length, width, hid_width):
    low, high = length // 2 - length // 16, length // 2 + length // 16
    tile = high // 3
    return {
        "wg": pltpu.VMEM((width, hid_width), BF16),
        "wu": pltpu.VMEM((width, hid_width), BF16),
        "wd": pltpu.VMEM((hid_width, width), BF16),
        "wdt": pltpu.VMEM((width, hid_width), BF16),
        "target": pltpu.VMEM((high, width), BF16),
        "target_t": pltpu.VMEM((width, high), BF16),
        "k_t": pltpu.VMEM((width, high), BF16),
        "hid": pltpu.VMEM((high, hid_width), BF16),
        "d_gate": pltpu.VMEM((high, hid_width), BF16),
        "d_up": pltpu.VMEM((high, hid_width), BF16),
        "grad": pltpu.VMEM((3, width, hid_width), F32),
        "x": pltpu.VMEM((3, width, hid_width), BF16),
        "y": pltpu.VMEM((3, width, hid_width), BF16),
        "a": pltpu.VMEM((3, width, width), BF16),
        "p": pltpu.VMEM((3, width, width), BF16),
        "apply_hid": pltpu.VMEM((tile, hid_width), BF16),
        "raw": pltpu.VMEM((tile, width), F32),
        "mid": pltpu.VMEM((high - low, width), F32),
        "w_sem": pltpu.SemaphoreType.DMA((3,)),
    }


def sizes(length, width, hid_width, rows):
    low, high = length // 2 - length // 16, length // 2 + length // 16
    return dict(
        length=length, width=width, hid_width=hid_width, rows=rows, low=low, high=high, tile=high // 3
    )


def compute_kernel(
    names, dims, group, bounds, q, k, v, rates, gain, gate_all, up_all, down_all, out, *scratch
):
    c = SimpleNamespace(**dims, **dict(zip(names, scratch)))
    tok, column = lax.axis_index("tok"), lax.axis_index("head")
    parity = tok % 2
    copies = [
        pltpu.make_async_copy(whole.at[parity], mine, c.w_sem.at[i])
        for i, (whole, mine) in enumerate(((gate_all, c.wg), (up_all, c.wu), (down_all, c.wd)))
    ]
    for copy in copies:
        copy.start()
    c.q, c.k, c.v, c.rates, c.out = q, k, v, rates, out
    c.gain = gain[2 * column + parity]
    c.bound = bounds[tok // 2]
    c.first_segment = jnp.where(tok < 2, 1, 0)
    for copy in copies:
        copy.wait()
    transpose_down(c)
    make_targets(c)
    backward(c)
    gradients(c)
    newton(c)
    renorm(c)
    attention(c)
    apply_old(c)
    for i in range(3):
        apply_new(c, i)


def flip(index, distance, count):
    result, place = 0, 1
    while place < count:
        bit = (index // place) % 2
        result = result + place * (1 - bit if distance & place else bit)
        place *= 2
    return result


def distances(peers):
    return sorted(range(1, peers), key=lambda d: (d < 2, d % 2, d))


def place_of(peer, tok, group):
    return (tok - tok % 2 + peer // group, peer % group)


def feature_of(peer, group):
    return 2 * (peer % group) + peer // group


def greet(others):
    barrier = pltpu.get_barrier_semaphore()
    for other in others:
        pl.semaphore_signal(barrier, inc=1, device_id=other, device_id_type=MESH)
    pl.semaphore_wait(barrier, len(others))


def gather_kernel(
    group, toks, width, q, k, v, r, oq, ok, ov, orate, send, recv, own_sem, halo_send, halo_recv
):
    tok, column = lax.axis_index("tok"), lax.axis_index("head")
    peers = 2 * group
    me = (tok % 2) * group + column
    after = ((tok + 2) % toks, column)
    before = ((tok + toks - 2) % toks, column)
    rows = q.shape[0]
    reach = WINDOW // rows
    greet([place_of(flip(me, d, peers), tok, group) for d in range(1, peers)] + [after, before])

    def source(t, peer):
        j = feature_of(peer, group)
        if t == 3:
            return r.at[j]
        return (k, v, q)[t].at[:, at(j * width, width, width)]

    def slot(t, peer):
        return (ok.at[reach + peer], ov.at[reach + peer], oq.at[peer], orate.at[peer])[t]

    def remote(t, d):
        peer = flip(me, d, peers)
        return pltpu.make_async_remote_copy(
            source(t, peer), slot(t, me), send.at[t, d], recv.at[t, d],
            device_id=place_of(peer, tok, group), device_id_type=MESH,
        )

    def arrival(t, d):
        peer = flip(me, d, peers)
        return pltpu.make_async_remote_copy(
            slot(t, peer), slot(t, peer), send.at[t, d], recv.at[t, d],
            device_id=place_of(peer, tok, group), device_id_type=MESH,
        )

    own = [pltpu.make_async_copy(source(t, me), slot(t, me), own_sem.at[t]) for t in range(4)]
    for t in (3, 0, 1, 2):
        for d in distances(peers):
            remote(t, d).start()
        own[t].start()
    for t in (3, 0, 1):
        for d in distances(peers):
            arrival(t, d).wait_recv()
        own[t].wait()
    halos = [
        pltpu.make_async_remote_copy(
            o.at[pl.ds(peers, reach)], o.at[pl.ds(0, reach)], halo_send.at[t], halo_recv.at[t],
            device_id=after, device_id_type=MESH,
        )
        for t, o in enumerate((ok, ov))
    ]
    for halo in halos:
        halo.start()
    for d in distances(peers):
        arrival(2, d).wait_recv()
    own[2].wait()
    for halo in halos:
        halo.wait()
    for t in range(4):
        for d in distances(peers):
            remote(t, d).wait_send()


def scatter_kernel(group, item, out, send, recv, own_sem):
    tok, column = lax.axis_index("tok"), lax.axis_index("head")
    peers = 2 * group
    me = (tok % 2) * group + column
    width = item.shape[2]
    greet([place_of(flip(me, d, peers), tok, group) for d in range(1, peers)])

    def block(peer):
        return out.at[:, at(feature_of(peer, group) * width, width, width)]

    def remote(d):
        peer = flip(me, d, peers)
        return pltpu.make_async_remote_copy(
            item.at[peer], block(me), send.at[d], recv.at[d],
            device_id=place_of(peer, tok, group), device_id_type=MESH,
        )

    def arrival(d):
        peer = flip(me, d, peers)
        return pltpu.make_async_remote_copy(
            item.at[peer], block(peer), send.at[d], recv.at[d],
            device_id=place_of(peer, tok, group), device_id_type=MESH,
        )

    own = pltpu.make_async_copy(item.at[me], block(me), own_sem)
    own.start()
    for d in distances(peers):
        remote(d).start()
    own.wait()
    for d in distances(peers):
        arrival(d).wait_recv()
    for d in distances(peers):
        remote(d).wait_send()


def body(queries, keys, values, token_rates, gate_start, up_start, down_start, norm_gain, bounds):
    rows, feats = queries.shape
    group, toks = lax.axis_size("head"), lax.axis_size("tok")
    heads, width, hid_width = token_rates.shape[1], gate_start.shape[1], gate_start.shape[2]
    peers = 2 * group
    length = peers * rows
    reach = WINDOW // rows
    anywhere = pl.BlockSpec(memory_space=pl.ANY)
    vmem = pl.BlockSpec(memory_space=pltpu.VMEM)
    dma = pltpu.SemaphoreType.DMA
    rates = jnp.broadcast_to(token_rates.T.astype(F32)[:, None, :], (heads, 8, rows))
    blocks = jax.ShapeDtypeStruct((peers, rows, width), BF16)
    wide = jax.ShapeDtypeStruct((reach + peers, rows, width), BF16)
    item_q, item_k, item_v, item_r = pl.pallas_call(
        functools.partial(gather_kernel, group, toks, width),
        out_shape=(blocks, wide, wide, jax.ShapeDtypeStruct((peers, 8, rows), F32)),
        in_specs=[anywhere] * 4,
        out_specs=[anywhere] * 4,
        scratch_shapes=[dma((4, peers)), dma((4, peers)), dma((4,)), dma((2,)), dma((2,))],
        compiler_params=pltpu.CompilerParams(collective_id=0, has_side_effects=True),
        name="gather",
    )(queries, keys, values, rates)
    scratch = scratch_of(length, width, hid_width)
    item = pl.pallas_call(
        functools.partial(
            compute_kernel, tuple(scratch), sizes(length, width, hid_width, rows), group
        ),
        out_shape=jax.ShapeDtypeStruct((length, width), BF16),
        in_specs=[pl.BlockSpec(memory_space=pltpu.SMEM)] + [vmem] * 5 + [anywhere] * 3,
        out_specs=vmem,
        scratch_shapes=list(scratch.values()),
        compiler_params=pltpu.CompilerParams(vmem_limit_bytes=64000000),
        name="compute",
    )(
        bounds,
        item_q.reshape(length, width),
        item_k.reshape(-1, width),
        item_v.reshape(-1, width),
        item_r,
        norm_gain.reshape(heads, 1, width),
        gate_start,
        up_start,
        down_start,
    )
    return pl.pallas_call(
        functools.partial(scatter_kernel, group),
        out_shape=jax.ShapeDtypeStruct((rows, feats), BF16),
        in_specs=[anywhere],
        out_specs=anywhere,
        scratch_shapes=[dma((peers,)), dma((peers,)), dma],
        compiler_params=pltpu.CompilerParams(collective_id=1, has_side_effects=True),
        name="scatter",
    )(item.reshape(peers, rows, width))


def solution(mesh):
    spread = P(("tok", "head"), None)
    owned = P("head", None, None)
    return jax.shard_map(
        body,
        mesh=mesh,
        in_specs=(spread,) * 4 + (owned,) * 3 + (P(), P()),
        out_specs=spread,
        check_vma=False,
    )
```

```python
import functools
import math
from types import SimpleNamespace

import jax
import jax.numpy as jnp
from jax import lax
from jax.experimental import pallas as pl
from jax.experimental.pallas import tpu as pltpu
from jax.sharding import PartitionSpec as P

AHD = 128
WINDOW = 512
NS_ITERS = 3
CHUNK = 256

linear_coef = 3.4445
cubic_coef = -4.775
quintic_coef = 2.0315
rms_epsilon = 1e-05
norm_epsilon = 1e-06
MESH = pl.DeviceIdType.MESH
F32 = jnp.float32
BF16 = jnp.bfloat16


def mm(a, b, ca=1, cb=0):
    return lax.dot_general(a, b, (((ca,), (cb,)), ((), ())), preferred_element_type=F32)


def logistic(x):
    return 0.5 * jnp.tanh(0.5 * x) + 0.5


def loop(count, fn):
    def step(i, carry):
        fn(i)
        return carry

    lax.fori_loop(0, count, step, 0)


def at(start, size, multiple):
    return pl.ds(pl.multiple_of(start, multiple), size)


def transpose_down(c):
    def step(i):
        cols = at(i * CHUNK, CHUNK, CHUNK)
        c.wdt[:, cols] = c.wd[cols, :].T

    loop(c.hid_width // CHUNK, step)


def transpose_keys(c):
    def step(i):
        c.k_t[:, at(i * 128, 128, 128)] = c.k[at(WINDOW + i * 128, 128, 128), :].T

    loop(c.high // 128, step)


def make_targets(c):
    per_block = c.rows // 128

    def step(i):
        rates = c.rates[i // per_block, 0:1, at((i % per_block) * 128, 128, 128)]
        rate_col = jnp.broadcast_to(rates, (128, 128)).T[:, 0:1]
        values = c.v[at(WINDOW + i * 128, 128, 128), :].astype(F32)
        place = i * 128 + lax.broadcasted_iota(jnp.int32, (128, c.width), 0)
        target = jnp.where(place < c.bound, rate_col * values, 0.0)
        c.target[at(i * 128, 128, 128), :] = target.astype(BF16)
        c.target_t[:, at(i * 128, 128, 128)] = target.T.astype(BF16)

    loop(c.high // 128, step)


def forward(c):
    chunks = c.hid_width // CHUNK

    def step(i):
        rows = at((i // chunks) * c.tile, c.tile, 128)
        cols = at((i % chunks) * CHUNK, CHUNK, CHUNK)
        k_rows = c.k[at(WINDOW + (i // chunks) * c.tile, c.tile, 128), :]
        gate = mm(k_rows, c.wg[:, cols])
        up = mm(k_rows, c.wu[:, cols])
        sig = logistic(gate)
        act = gate * sig
        c.hid[rows, cols] = (act * up).astype(BF16)
        c.act[rows, cols] = act
        c.slope[rows, cols] = up * (sig + act * (1.0 - sig))

    loop((c.high // c.tile) * chunks, step)


def backward(c):
    chunks = c.hid_width // CHUNK

    def step(i):
        rows = at((i // chunks) * c.tile, c.tile, 128)
        cols = at((i % chunks) * CHUNK, CHUNK, CHUNK)
        back = mm(c.target[rows, :], c.wdt[:, cols])
        c.d_gate[rows, cols] = (back * c.slope[rows, cols]).astype(BF16)
        c.d_up[rows, cols] = (back * c.act[rows, cols]).astype(BF16)

    loop((c.high // c.tile) * chunks, step)


def gradients(c):
    def step(i):
        cols = at(i * CHUNK, CHUNK, CHUNK)
        c.grad[0, :, cols] = mm(c.k_t[...], c.d_gate[:, cols])
        c.grad[1, :, cols] = mm(c.k_t[...], c.d_up[:, cols])
        c.grad[2, :, cols] = mm(c.target_t[...], c.hid[:, cols])

    loop(c.hid_width // CHUNK, step)

    def scale(m):
        grad = c.grad[m]
        frob = lax.rsqrt(jnp.sum(grad * grad, keepdims=True) + norm_epsilon)
        c.x[0, m] = (grad * frob).astype(BF16)

    loop(3, scale)


def newton(c):
    def sweep(turn):
        old, new = turn % 2, (turn + 1) % 2
        for m in range(3):
            x = c.x[old, m]
            c.a[m] = mm(x, x, 1, 1).astype(BF16)
        for m in range(3):
            a = c.a[m]
            c.p[m] = (cubic_coef * a.astype(F32) + quintic_coef * mm(a, a)).astype(BF16)
        for m in range(3):
            x = c.x[old, m]
            c.x[new, m] = (linear_coef * x.astype(F32) + mm(c.p[m], x)).astype(BF16)

    loop(NS_ITERS, sweep)


def renorm(c):
    def by_column(i):
        cols = at(i * CHUNK, CHUNK, CHUNK)
        for m, ref in ((0, c.wg), (1, c.wu)):
            w = ref[:, cols].astype(F32)
            u = w + c.x[NS_ITERS % 2, m, :, cols].astype(F32)
            want = jnp.sqrt(jnp.sum(w * w, axis=0, keepdims=True) + norm_epsilon)
            have = jnp.sqrt(jnp.sum(u * u, axis=0, keepdims=True) + norm_epsilon)
            c.x[NS_ITERS % 2, m, :, cols] = (u * (want / have)).astype(BF16)

    loop(c.hid_width // CHUNK, by_column)

    def by_row(i):
        rows = at(i * 128, 128, 128)
        w = c.wdt[rows, :].astype(F32)
        u = w + c.x[NS_ITERS % 2, 2, rows, :].astype(F32)
        want = jnp.sqrt(jnp.sum(w * w, axis=1, keepdims=True) + norm_epsilon)
        have = jnp.sqrt(jnp.sum(u * u, axis=1, keepdims=True) + norm_epsilon)
        c.x[NS_ITERS % 2, 2, rows, :] = (u * (want / have)).astype(BF16)

    loop(c.width // 128, by_row)


def attention(c, first, count):
    tile = WINDOW // 2
    power = math.log2(math.e) / math.sqrt(AHD)

    def step(i):
        t = first + i
        rows = at(t * tile, tile, tile)
        span = at(t * tile, WINDOW + tile, tile)
        below = lax.broadcasted_iota(jnp.int32, (tile, tile), 1) <= lax.broadcasted_iota(
            jnp.int32, (tile, tile), 0
        )
        far_bias = jnp.where(c.first_segment * (2 - t) > 0, F32(-1e30), F32(0.0))
        mid_bias = jnp.where(c.first_segment * (1 - t) > 0, F32(-1e30), F32(0.0))
        for head in range(c.width // AHD):
            feats = slice(head * AHD, (head + 1) * AHD)
            scores = mm(c.q[rows, feats], c.k[span, feats], 1, 1)
            edge = jnp.where(below, scores[:, 2 * tile :], scores[:, :tile] + far_bias)
            mid = scores[:, tile : 2 * tile] + mid_bias
            top = jnp.max(jnp.maximum(edge, mid), axis=1, keepdims=True)
            edge = jnp.exp2((edge - top) * power)
            mid = jnp.exp2((mid - top) * power)
            total = jnp.sum(edge + mid, axis=1, keepdims=True)
            weights = jnp.concatenate(
                [
                    jnp.where(below, 0.0, edge).astype(BF16),
                    mid.astype(BF16),
                    jnp.where(below, edge, 0.0).astype(BF16),
                ],
                axis=1,
            )
            mixed = mm(weights, c.v[span, feats])
            c.out[rows, feats] = (mixed / total).astype(BF16)

    loop(count, step)


def swiglu(c, start, gate, up, down, down_dim):
    q_rows = c.q[at(start, c.rows, c.rows), :]

    def step(i):
        cols = at(i * CHUNK, CHUNK, CHUNK)
        pre_gate = mm(q_rows, gate[:, cols])
        pre_up = mm(q_rows, up[:, cols])
        c.apply_hid[:, cols] = (pre_gate * logistic(pre_gate) * pre_up).astype(BF16)

    loop(c.hid_width // CHUNK, step)
    return mm(c.apply_hid[...], down[...], 1, down_dim)


def fast_rows(c, start):
    new = c.x.at[NS_ITERS % 2]

    @pl.when(start < c.high)
    def _():
        c.raw[...] = swiglu(c, start, c.wg, c.wu, c.wd, 0)

    @pl.when(start + c.rows > c.low)
    def _():
        after = swiglu(c, start, new.at[0], new.at[1], new.at[2], 1)
        place = start + lax.broadcasted_iota(jnp.int32, after.shape, 0)
        kept = (place < c.bound) & (place < c.high)
        c.raw[...] = jnp.where(kept, c.raw[...], after)

    raw = c.raw[...]
    rows = at(start, c.rows, c.rows)
    scale = lax.rsqrt(jnp.mean(raw * raw, axis=1, keepdims=True) + rms_epsilon)
    fast = (raw * scale * c.gain).astype(BF16)
    c.out[rows, :] = (c.out[rows, :].astype(F32) + fast.astype(F32)).astype(BF16)


def scratch_of(length, width, hid_width, rows, peers):
    low, high = length // 2 - length // 16, length // 2 + length // 16
    dma = pltpu.SemaphoreType.DMA
    return {
        "q": pltpu.VMEM((length, width), BF16),
        "k": pltpu.VMEM((WINDOW + length, width), BF16),
        "v": pltpu.VMEM((WINDOW + length, width), BF16),
        "rates": pltpu.VMEM((peers, 8, rows), F32),
        "out": pltpu.VMEM((length, width), BF16),
        "send": dma((4, peers)),
        "recv": dma((4, peers)),
        "own_sem": dma((4,)),
        "halo_send": dma((2,)),
        "halo_recv": dma((2,)),
        "out_send": dma((peers,)),
        "out_recv": dma((peers,)),
        "out_own": dma,
        "wg": pltpu.VMEM((width, hid_width), BF16),
        "wu": pltpu.VMEM((width, hid_width), BF16),
        "wd": pltpu.VMEM((hid_width, width), BF16),
        "wdt": pltpu.VMEM((width, hid_width), BF16),
        "target": pltpu.VMEM((high, width), BF16),
        "target_t": pltpu.VMEM((width, high), BF16),
        "k_t": pltpu.VMEM((width, high), BF16),
        "hid": pltpu.VMEM((high, hid_width), BF16),
        "d_gate": pltpu.VMEM((high, hid_width), BF16),
        "d_up": pltpu.VMEM((high, hid_width), BF16),
        "grad": pltpu.VMEM((3, width, hid_width), F32),
        "x": pltpu.VMEM((2, 3, width, hid_width), BF16),
        "act": pltpu.VMEM((high, hid_width), F32),
        "slope": pltpu.VMEM((high, hid_width), F32),
        "a": pltpu.VMEM((3, width, width), BF16),
        "p": pltpu.VMEM((3, width, width), BF16),
        "apply_hid": pltpu.VMEM((rows, hid_width), BF16),
        "raw": pltpu.VMEM((rows, width), F32),
        "w_sem": dma((3,)),
    }


def sizes(length, width, hid_width, rows):
    low, high = length // 2 - length // 16, length // 2 + length // 16
    return dict(
        length=length, width=width, hid_width=hid_width, rows=rows, low=low, high=high, tile=high // 3
    )


def flip(index, distance, count):
    result, place = 0, 1
    while place < count:
        bit = (index // place) % 2
        result = result + place * (1 - bit if distance & place else bit)
        place *= 2
    return result


def distances(peers):
    return sorted(range(1, peers), key=lambda d: (d < 2, d % 2, d))


def order_of(step, peers):
    half = peers // 2
    return jnp.where(
        step < half - 1, 2 * step + 2, jnp.where(step < peers - 2, 2 * (step - half) + 5, peers - 1 - step)
    )


def flip_by(index, distance, count):
    result, place = 0, 1
    while place < count:
        bit, other = (index // place) % 2, (distance // place) % 2
        result = result + place * (bit + other - 2 * bit * other)
        place *= 2
    return result


def place_of(peer, tok, group):
    return (tok - tok % 2 + peer // group, peer % group)


def feature_of(peer, group):
    return 2 * (peer % group) + peer // group


def greet(others):
    barrier = pltpu.get_barrier_semaphore()
    for other in others:
        pl.semaphore_signal(barrier, inc=1, device_id=other, device_id_type=MESH)
    pl.semaphore_wait(barrier, len(others))


def kernel(
    names, dims, group, toks, bounds, gain, q, k, v, r, gate_all, up_all, down_all, out, *scratch
):
    c = SimpleNamespace(**dims, **dict(zip(names, scratch)))
    tok, column = lax.axis_index("tok"), lax.axis_index("head")
    parity = tok % 2
    peers, rows, width = 2 * group, c.rows, c.width
    me = parity * group + column
    after = ((tok + 2) % toks, column)
    before = ((tok + toks - 2) % toks, column)
    weights = [
        pltpu.make_async_copy(whole.at[parity], mine, c.w_sem.at[i])
        for i, (whole, mine) in enumerate(((gate_all, c.wg), (up_all, c.wu), (down_all, c.wd)))
    ]
    for copy in weights:
        copy.start()
    c.gain = gain[2 * column + parity]
    c.bound = bounds[tok // 2]
    c.first_segment = jnp.where(tok < 2, 1, 0)
    greet([place_of(flip(me, d, peers), tok, group) for d in range(1, peers)] + [after, before])

    def source(t, peer):
        j = feature_of(peer, group)
        if t == 3:
            return r.at[j]
        return (k, v, q)[t].at[:, at(j * width, width, width)]

    def slot(t, peer):
        if t == 3:
            return c.rates.at[peer]
        shift = WINDOW if t < 2 else 0
        return (c.k, c.v, c.q)[t].at[at(shift + peer * rows, rows, rows), :]

    def remote(t, peer):
        return pltpu.make_async_remote_copy(
            source(t, peer), slot(t, me), c.send.at[t, peer], c.recv.at[t, me],
            device_id=place_of(peer, tok, group), device_id_type=MESH,
        )

    def own(t):
        return pltpu.make_async_copy(source(t, me), slot(t, me), c.own_sem.at[t])

    def arrived(t, peer):
        @pl.when(me != peer)
        def _():
            pltpu.make_async_remote_copy(
                slot(t, peer), slot(t, peer), c.send.at[t, peer], c.recv.at[t, peer],
                device_id=place_of(peer, tok, group), device_id_type=MESH,
            ).wait_recv()

        @pl.when(me == peer)
        def _():
            own(t).wait()

    def block(peer):
        return out.at[:, at(feature_of(peer, group) * width, width, width)]

    def done_rows(peer):
        return c.out.at[at(peer * rows, rows, rows), :]

    def give(peer):
        return pltpu.make_async_remote_copy(
            done_rows(peer), block(me), c.out_send.at[peer], c.out_recv.at[me],
            device_id=place_of(peer, tok, group), device_id_type=MESH,
        )

    def taken(peer):
        return pltpu.make_async_remote_copy(
            done_rows(peer), block(peer), c.out_send.at[peer], c.out_recv.at[peer],
            device_id=place_of(peer, tok, group), device_id_type=MESH,
        )

    order = distances(peers)
    for t in (3, 0, 1, 2):
        for d in order:
            remote(t, flip(me, d, peers)).start()
        own(t).start()
    for copy in weights:
        copy.wait()
    transpose_down(c)
    needed = -(-c.high // rows)
    for p in range(needed):
        arrived(0, p)
    forward(c)
    transpose_keys(c)
    for p in range(peers):
        arrived(3, p)
    for p in range(needed):
        arrived(1, p)
    make_targets(c)
    backward(c)
    gradients(c)
    for t in (0, 1):
        for p in range(needed, peers):
            arrived(t, p)
    halos = [
        pltpu.make_async_remote_copy(
            o.at[pl.ds(c.length, WINDOW), :], o.at[pl.ds(0, WINDOW), :],
            c.halo_send.at[t], c.halo_recv.at[t], device_id=after, device_id_type=MESH,
        )
        for t, o in enumerate((c.k, c.v))
    ]
    for halo in halos:
        halo.start()
    newton(c)
    renorm(c)
    for p in range(peers):
        arrived(2, p)
    for halo in halos:
        halo.wait()
    tiles = rows // (WINDOW // 2)

    def turn(step):
        peer = flip_by(me, order_of(step, peers), peers)
        attention(c, peer * tiles, tiles)
        fast_rows(c, peer * rows)

        @pl.when(peer != me)
        def _():
            give(peer).start()

        @pl.when(peer == me)
        def _():
            pltpu.make_async_copy(done_rows(me), block(me), c.out_own).start()

    loop(peers, turn)
    pltpu.make_async_copy(done_rows(me), block(me), c.out_own).wait()
    for d in order:
        taken(flip(me, d, peers)).wait_recv()
    for d in order:
        give(flip(me, d, peers)).wait_send()
        for t in range(4):
            remote(t, flip(me, d, peers)).wait_send()


def body(queries, keys, values, token_rates, gate_start, up_start, down_start, norm_gain, bounds):
    rows, feats = queries.shape
    group, toks = lax.axis_size("head"), lax.axis_size("tok")
    heads, width, hid_width = token_rates.shape[1], gate_start.shape[1], gate_start.shape[2]
    peers = 2 * group
    length = peers * rows
    anywhere = pl.BlockSpec(memory_space=pl.ANY)
    vmem = pl.BlockSpec(memory_space=pltpu.VMEM)
    dma = pltpu.SemaphoreType.DMA
    rates = jnp.broadcast_to(token_rates.T.astype(F32)[:, None, :], (heads, 8, rows))
    scratch = scratch_of(length, width, hid_width, rows, peers)
    return pl.pallas_call(
        functools.partial(
            kernel, tuple(scratch), sizes(length, width, hid_width, rows), group, toks
        ),
        out_shape=jax.ShapeDtypeStruct((rows, feats), BF16),
        in_specs=[pl.BlockSpec(memory_space=pltpu.SMEM), vmem] + [anywhere] * 7,
        out_specs=anywhere,
        scratch_shapes=list(scratch.values()),
        compiler_params=pltpu.CompilerParams(
            collective_id=0, has_side_effects=True, vmem_limit_bytes=66000000
        ),
        name="layer",
    )(
        bounds, norm_gain.reshape(heads, 1, width), queries, keys, values, rates,
        gate_start, up_start, down_start,
    )


def solution(mesh):
    spread = P(("tok", "head"), None)
    owned = P("head", None, None)
    return jax.shard_map(
        body,
        mesh=mesh,
        in_specs=(spread,) * 4 + (owned,) * 3 + (P(), P()),
        out_specs=spread,
        check_vma=False,
    )
```

```python
import functools
import math
from types import SimpleNamespace

import jax
import jax.numpy as jnp
from jax import lax
from jax.experimental import pallas as pl
from jax.experimental.pallas import tpu as pltpu
from jax.sharding import PartitionSpec as P

AHD = 128
WINDOW = 512
NS_ITERS = 3
CHUNK = 512

linear_coef = 3.4445
cubic_coef = -4.775
quintic_coef = 2.0315
rms_epsilon = 1e-05
norm_epsilon = 1e-06
MESH = pl.DeviceIdType.MESH
F32 = jnp.float32
BF16 = jnp.bfloat16


def mm(a, b, ca=1, cb=0):
    return lax.dot_general(a, b, (((ca,), (cb,)), ((), ())), preferred_element_type=F32)


def logistic(x):
    return 0.5 * jnp.tanh(0.5 * x) + 0.5


def loop(count, fn):
    def step(i, carry):
        fn(i)
        return carry

    lax.fori_loop(0, count, step, 0)


def at(start, size, multiple):
    return pl.ds(pl.multiple_of(start, multiple), size)


def transpose_down(c):
    def step(i):
        cols = at(i * CHUNK, CHUNK, CHUNK)
        c.wdt[:, cols] = c.wd[cols, :].T

    loop(c.hid_width // CHUNK, step)


def transpose_keys(c):
    def step(i):
        c.k_t[:, at(i * 128, 128, 128)] = c.k[at(WINDOW + i * 128, 128, 128), :].T

    loop(c.high // 128, step)


def make_targets(c):
    per_block = c.rows // 128

    def step(i):
        rates = c.rates[i // per_block, 0:1, at((i % per_block) * 128, 128, 128)]
        rate_col = jnp.broadcast_to(rates, (128, 128)).T[:, 0:1]
        values = c.v[at(WINDOW + i * 128, 128, 128), :].astype(F32)
        place = i * 128 + lax.broadcasted_iota(jnp.int32, (128, c.width), 0)
        target = jnp.where(place < c.bound, rate_col * values, 0.0)
        c.target[at(i * 128, 128, 128), :] = target.astype(BF16)
        c.target_t[:, at(i * 128, 128, 128)] = target.T.astype(BF16)

    loop(c.high // 128, step)


def forward(c):
    chunks = c.hid_width // CHUNK

    def step(i):
        rows = at((i // chunks) * c.tile, c.tile, 128)
        cols = at((i % chunks) * CHUNK, CHUNK, CHUNK)
        k_rows = c.k[at(WINDOW + (i // chunks) * c.tile, c.tile, 128), :]
        gate = mm(k_rows, c.wg[:, cols])
        up = mm(k_rows, c.wu[:, cols])
        sig = logistic(gate)
        act = gate * sig
        c.hid[rows, cols] = (act * up).astype(BF16)
        c.act[rows, cols] = act
        c.slope[rows, cols] = up * (sig + act * (1.0 - sig))

    loop((c.high // c.tile) * chunks, step)


def backward(c):
    chunks = c.hid_width // CHUNK

    def step(i):
        rows = at((i // chunks) * c.tile, c.tile, 128)
        cols = at((i % chunks) * CHUNK, CHUNK, CHUNK)
        back = mm(c.target[rows, :], c.wdt[:, cols])
        c.d_gate[rows, cols] = (back * c.slope[rows, cols]).astype(BF16)
        c.d_up[rows, cols] = (back * c.act[rows, cols]).astype(BF16)

    loop((c.high // c.tile) * chunks, step)


def gradients(c):
    def step(i):
        cols = at(i * CHUNK, CHUNK, CHUNK)
        c.grad[0, :, cols] = mm(c.k_t[...], c.d_gate[:, cols])
        c.grad[1, :, cols] = mm(c.k_t[...], c.d_up[:, cols])
        c.grad[2, :, cols] = mm(c.target_t[...], c.hid[:, cols])

    loop(c.hid_width // CHUNK, step)

    def scale(m):
        grad = c.grad[m]
        frob = lax.rsqrt(jnp.sum(grad * grad, keepdims=True) + norm_epsilon)
        c.x[0, m] = (grad * frob).astype(BF16)

    loop(3, scale)


def newton(c):
    def sweep(turn):
        old, new = turn % 2, (turn + 1) % 2
        for m in range(3):
            x = c.x[old, m]
            c.a[m] = mm(x, x, 1, 1).astype(BF16)
        for m in range(3):
            a = c.a[m]
            c.p[m] = (cubic_coef * a.astype(F32) + quintic_coef * mm(a, a)).astype(BF16)
        for m in range(3):
            x = c.x[old, m]
            c.x[new, m] = (linear_coef * x.astype(F32) + mm(c.p[m], x)).astype(BF16)

    loop(NS_ITERS, sweep)


def renorm(c):
    def by_column(i):
        cols = at(i * CHUNK, CHUNK, CHUNK)
        for m, ref in ((0, c.wg), (1, c.wu)):
            w = ref[:, cols].astype(F32)
            u = w + c.x[NS_ITERS % 2, m, :, cols].astype(F32)
            want = jnp.sqrt(jnp.sum(w * w, axis=0, keepdims=True) + norm_epsilon)
            have = jnp.sqrt(jnp.sum(u * u, axis=0, keepdims=True) + norm_epsilon)
            c.x[NS_ITERS % 2, m, :, cols] = (u * (want / have)).astype(BF16)

    loop(c.hid_width // CHUNK, by_column)

    def by_row(i):
        rows = at(i * 128, 128, 128)
        w = c.wdt[rows, :].astype(F32)
        u = w + c.x[NS_ITERS % 2, 2, rows, :].astype(F32)
        want = jnp.sqrt(jnp.sum(w * w, axis=1, keepdims=True) + norm_epsilon)
        have = jnp.sqrt(jnp.sum(u * u, axis=1, keepdims=True) + norm_epsilon)
        c.x[NS_ITERS % 2, 2, rows, :] = (u * (want / have)).astype(BF16)

    loop(c.width // 128, by_row)


def attention(c, first, count):
    tile = WINDOW // 2
    power = math.log2(math.e) / math.sqrt(AHD)

    def step(i):
        t = first + i
        rows = at(t * tile, tile, tile)
        span = at(t * tile, WINDOW + tile, tile)
        below = lax.broadcasted_iota(jnp.int32, (tile, tile), 1) <= lax.broadcasted_iota(
            jnp.int32, (tile, tile), 0
        )
        far_bias = jnp.where(c.first_segment * (2 - t) > 0, F32(-1e30), F32(0.0))
        mid_bias = jnp.where(c.first_segment * (1 - t) > 0, F32(-1e30), F32(0.0))
        for head in range(c.width // AHD):
            feats = slice(head * AHD, (head + 1) * AHD)
            scores = mm(c.q[rows, feats], c.k[span, feats], 1, 1)
            edge = jnp.where(below, scores[:, 2 * tile :], scores[:, :tile] + far_bias)
            mid = scores[:, tile : 2 * tile] + mid_bias
            top = jnp.max(jnp.maximum(edge, mid), axis=1, keepdims=True)
            edge = jnp.exp2((edge - top) * power)
            mid = jnp.exp2((mid - top) * power)
            total = jnp.sum(edge + mid, axis=1, keepdims=True)
            weights = jnp.concatenate(
                [
                    jnp.where(below, 0.0, edge).astype(BF16),
                    mid.astype(BF16),
                    jnp.where(below, edge, 0.0).astype(BF16),
                ],
                axis=1,
            )
            mixed = mm(weights, c.v[span, feats])
            c.out[rows, feats] = (mixed / total).astype(BF16)

    loop(count, step)


def swiglu(c, start, gate, up, down, down_dim):
    q_rows = c.q[at(start, c.rows, c.rows), :]

    def step(i):
        cols = at(i * CHUNK, CHUNK, CHUNK)
        pre_gate = mm(q_rows, gate[:, cols])
        pre_up = mm(q_rows, up[:, cols])
        c.apply_hid[:, cols] = (pre_gate * logistic(pre_gate) * pre_up).astype(BF16)

    loop(c.hid_width // CHUNK, step)
    return mm(c.apply_hid[...], down[...], 1, down_dim)


def fast_rows(c, start):
    new = c.x.at[NS_ITERS % 2]

    @pl.when(start < c.high)
    def _():
        c.raw[...] = swiglu(c, start, c.wg, c.wu, c.wd, 0)

    @pl.when(start + c.rows > c.low)
    def _():
        after = swiglu(c, start, new.at[0], new.at[1], new.at[2], 1)
        place = start + lax.broadcasted_iota(jnp.int32, after.shape, 0)
        kept = (place < c.bound) & (place < c.high)
        c.raw[...] = jnp.where(kept, c.raw[...], after)

    raw = c.raw[...]
    rows = at(start, c.rows, c.rows)
    scale = lax.rsqrt(jnp.mean(raw * raw, axis=1, keepdims=True) + rms_epsilon)
    fast = (raw * scale * c.gain).astype(BF16)
    c.out[rows, :] = (c.out[rows, :].astype(F32) + fast.astype(F32)).astype(BF16)


def scratch_of(length, width, hid_width, rows, peers):
    low, high = length // 2 - length // 16, length // 2 + length // 16
    dma = pltpu.SemaphoreType.DMA
    return {
        "q": pltpu.VMEM((length, width), BF16),
        "k": pltpu.VMEM((WINDOW + length, width), BF16),
        "v": pltpu.VMEM((WINDOW + length, width), BF16),
        "rates": pltpu.VMEM((peers, 8, rows), F32),
        "out": pltpu.VMEM((length, width), BF16),
        "send": dma((4, peers)),
        "recv": dma((4, peers)),
        "own_sem": dma((4,)),
        "halo_send": dma((2,)),
        "halo_recv": dma((2,)),
        "out_send": dma((peers,)),
        "out_recv": dma((peers,)),
        "out_own": dma,
        "wg": pltpu.VMEM((width, hid_width), BF16),
        "wu": pltpu.VMEM((width, hid_width), BF16),
        "wd": pltpu.VMEM((hid_width, width), BF16),
        "wdt": pltpu.VMEM((width, hid_width), BF16),
        "target": pltpu.VMEM((high, width), BF16),
        "target_t": pltpu.VMEM((width, high), BF16),
        "k_t": pltpu.VMEM((width, high), BF16),
        "hid": pltpu.VMEM((high, hid_width), BF16),
        "d_gate": pltpu.VMEM((high, hid_width), BF16),
        "d_up": pltpu.VMEM((high, hid_width), BF16),
        "grad": pltpu.VMEM((3, width, hid_width), F32),
        "x": pltpu.VMEM((2, 3, width, hid_width), BF16),
        "act": pltpu.VMEM((high, hid_width), F32),
        "slope": pltpu.VMEM((high, hid_width), F32),
        "a": pltpu.VMEM((3, width, width), BF16),
        "p": pltpu.VMEM((3, width, width), BF16),
        "apply_hid": pltpu.VMEM((rows, hid_width), BF16),
        "raw": pltpu.VMEM((rows, width), F32),
        "w_sem": dma((3,)),
    }


def sizes(length, width, hid_width, rows):
    low, high = length // 2 - length // 16, length // 2 + length // 16
    return dict(
        length=length, width=width, hid_width=hid_width, rows=rows, low=low, high=high, tile=high // 3
    )


def flip(index, distance, count):
    result, place = 0, 1
    while place < count:
        bit = (index // place) % 2
        result = result + place * (1 - bit if distance & place else bit)
        place *= 2
    return result


def distances(peers):
    return sorted(range(1, peers), key=lambda d: (d > 1, d % 2, d))


def order_of(step, peers):
    half = peers // 2
    return jnp.where(
        step < half - 1, 2 * step + 2, jnp.where(step < peers - 2, 2 * (step - half) + 5, peers - 1 - step)
    )


def flip_by(index, distance, count):
    result, place = 0, 1
    while place < count:
        bit, other = (index // place) % 2, (distance // place) % 2
        result = result + place * (bit + other - 2 * bit * other)
        place *= 2
    return result


def place_of(peer, tok, group):
    return (tok - tok % 2 + peer // group, peer % group)


def feature_of(peer, group):
    return 2 * (peer % group) + peer // group


def greet(others):
    barrier = pltpu.get_barrier_semaphore()
    for other in others:
        pl.semaphore_signal(barrier, inc=1, device_id=other, device_id_type=MESH)
    pl.semaphore_wait(barrier, len(others))


def kernel(
    names, dims, group, toks, bounds, gain, q, k, v, r, gate_all, up_all, down_all, out, *scratch
):
    c = SimpleNamespace(**dims, **dict(zip(names, scratch)))
    tok, column = lax.axis_index("tok"), lax.axis_index("head")
    parity = tok % 2
    peers, rows, width = 2 * group, c.rows, c.width
    me = parity * group + column
    after = ((tok + 2) % toks, column)
    before = ((tok + toks - 2) % toks, column)
    weights = [
        pltpu.make_async_copy(whole.at[parity], mine, c.w_sem.at[i])
        for i, (whole, mine) in enumerate(((gate_all, c.wg), (up_all, c.wu), (down_all, c.wd)))
    ]
    for copy in weights:
        copy.start()
    c.gain = gain[2 * column + parity]
    c.bound = bounds[tok // 2]
    c.first_segment = jnp.where(tok < 2, 1, 0)
    greet([place_of(flip(me, d, peers), tok, group) for d in range(1, peers)] + [after, before])

    def source(t, peer):
        j = feature_of(peer, group)
        if t == 3:
            return r.at[j]
        return (k, v, q)[t].at[:, at(j * width, width, width)]

    def slot(t, peer):
        if t == 3:
            return c.rates.at[peer]
        shift = WINDOW if t < 2 else 0
        return (c.k, c.v, c.q)[t].at[at(shift + peer * rows, rows, rows), :]

    def remote(t, peer):
        return pltpu.make_async_remote_copy(
            source(t, peer), slot(t, me), c.send.at[t, peer], c.recv.at[t, me],
            device_id=place_of(peer, tok, group), device_id_type=MESH,
        )

    def own(t):
        return pltpu.make_async_copy(source(t, me), slot(t, me), c.own_sem.at[t])

    def arrived(t, peer):
        @pl.when(me != peer)
        def _():
            pltpu.make_async_remote_copy(
                slot(t, peer), slot(t, peer), c.send.at[t, peer], c.recv.at[t, peer],
                device_id=place_of(peer, tok, group), device_id_type=MESH,
            ).wait_recv()

        @pl.when(me == peer)
        def _():
            own(t).wait()

    def block(peer):
        return out.at[:, at(feature_of(peer, group) * width, width, width)]

    def done_rows(peer):
        return c.out.at[at(peer * rows, rows, rows), :]

    def give(peer):
        return pltpu.make_async_remote_copy(
            done_rows(peer), block(me), c.out_send.at[peer], c.out_recv.at[me],
            device_id=place_of(peer, tok, group), device_id_type=MESH,
        )

    def taken(peer):
        return pltpu.make_async_remote_copy(
            done_rows(peer), block(peer), c.out_send.at[peer], c.out_recv.at[peer],
            device_id=place_of(peer, tok, group), device_id_type=MESH,
        )

    order = distances(peers)
    for t in (3, 0):
        for d in order:
            remote(t, flip(me, d, peers)).start()
        own(t).start()

    def send_next(t):
        for d in order:
            remote(t - 1, flip(me, d, peers)).wait_send()
            remote(t, flip(me, d, peers)).start()
        own(t).start()

    for copy in weights:
        copy.wait()
    transpose_down(c)
    send_next(1)
    needed = -(-c.high // rows)
    for p in range(needed):
        arrived(0, p)
    forward(c)
    transpose_keys(c)
    send_next(2)
    for p in range(peers):
        arrived(3, p)
    for p in range(needed):
        arrived(1, p)
    make_targets(c)
    backward(c)
    gradients(c)
    for t in (0, 1):
        for p in range(needed, peers):
            arrived(t, p)
    halos = [
        pltpu.make_async_remote_copy(
            o.at[pl.ds(c.length, WINDOW), :], o.at[pl.ds(0, WINDOW), :],
            c.halo_send.at[t], c.halo_recv.at[t], device_id=after, device_id_type=MESH,
        )
        for t, o in enumerate((c.k, c.v))
    ]
    for halo in halos:
        halo.start()
    newton(c)
    renorm(c)
    for p in range(peers):
        arrived(2, p)
    for halo in halos:
        halo.wait()
    tiles = rows // (WINDOW // 2)

    def turn(step):
        peer = flip_by(me, order_of(step, peers), peers)
        attention(c, peer * tiles, tiles)
        fast_rows(c, peer * rows)

        @pl.when(peer != me)
        def _():
            give(peer).start()

        @pl.when(peer == me)
        def _():
            pltpu.make_async_copy(done_rows(me), block(me), c.out_own).start()

    loop(peers, turn)
    pltpu.make_async_copy(done_rows(me), block(me), c.out_own).wait()
    for d in order:
        taken(flip(me, d, peers)).wait_recv()
    for d in order:
        give(flip(me, d, peers)).wait_send()
        for t in (2, 3):
            remote(t, flip(me, d, peers)).wait_send()


def body(queries, keys, values, token_rates, gate_start, up_start, down_start, norm_gain, bounds):
    rows, feats = queries.shape
    group, toks = lax.axis_size("head"), lax.axis_size("tok")
    heads, width, hid_width = token_rates.shape[1], gate_start.shape[1], gate_start.shape[2]
    peers = 2 * group
    length = peers * rows
    anywhere = pl.BlockSpec(memory_space=pl.ANY)
    vmem = pl.BlockSpec(memory_space=pltpu.VMEM)
    dma = pltpu.SemaphoreType.DMA
    rates = jnp.broadcast_to(token_rates.T.astype(F32)[:, None, :], (heads, 8, rows))
    scratch = scratch_of(length, width, hid_width, rows, peers)
    return pl.pallas_call(
        functools.partial(
            kernel, tuple(scratch), sizes(length, width, hid_width, rows), group, toks
        ),
        out_shape=jax.ShapeDtypeStruct((rows, feats), BF16),
        in_specs=[pl.BlockSpec(memory_space=pltpu.SMEM), vmem] + [anywhere] * 7,
        out_specs=anywhere,
        scratch_shapes=list(scratch.values()),
        compiler_params=pltpu.CompilerParams(
            collective_id=0, has_side_effects=True, vmem_limit_bytes=66000000
        ),
        name="layer",
    )(
        bounds, norm_gain.reshape(heads, 1, width), queries, keys, values, rates,
        gate_start, up_start, down_start,
    )


def solution(mesh):
    spread = P(("tok", "head"), None)
    owned = P("head", None, None)
    return jax.shard_map(
        body,
        mesh=mesh,
        in_specs=(spread,) * 4 + (owned,) * 3 + (P(), P()),
        out_specs=spread,
        check_vma=False,
    )
```

```python
import functools
import math
from types import SimpleNamespace

import jax
import jax.numpy as jnp
from jax import lax
from jax.experimental import pallas as pl
from jax.experimental.pallas import tpu as pltpu
from jax.sharding import PartitionSpec as P

AHD = 128
WINDOW = 512
NS_ITERS = 3
CHUNK = 512

linear_coef = 3.4445
cubic_coef = -4.775
quintic_coef = 2.0315
rms_epsilon = 1e-05
norm_epsilon = 1e-06
MESH = pl.DeviceIdType.MESH
F32 = jnp.float32
BF16 = jnp.bfloat16


def mm(a, b, ca=1, cb=0):
    return lax.dot_general(a, b, (((ca,), (cb,)), ((), ())), preferred_element_type=F32)


def logistic(x):
    return 0.5 * jnp.tanh(0.5 * x) + 0.5


def loop(count, fn):
    def step(i, carry):
        fn(i)
        return carry

    lax.fori_loop(0, count, step, 0)


def at(start, size, multiple):
    return pl.ds(pl.multiple_of(start, multiple), size)


def transpose_down(c):
    def step(i):
        cols = at(i * CHUNK, CHUNK, CHUNK)
        c.wdt[:, cols] = c.wd[cols, :].T

    loop(c.hid_width // CHUNK, step)


def transpose_keys(c):
    def step(i):
        c.k_t[:, at(i * 128, 128, 128)] = c.k[at(WINDOW + i * 128, 128, 128), :].T

    loop(c.high // 128, step)


def make_targets(c):
    per_block = c.rows // 128

    def step(i):
        rates = c.rates[i // per_block, 0:1, at((i % per_block) * 128, 128, 128)]
        rate_col = jnp.broadcast_to(rates, (128, 128)).T[:, 0:1]
        values = c.v[at(WINDOW + i * 128, 128, 128), :].astype(F32)
        place = i * 128 + lax.broadcasted_iota(jnp.int32, (128, c.width), 0)
        target = jnp.where(place < c.bound, rate_col * values, 0.0)
        c.target[at(i * 128, 128, 128), :] = target.astype(BF16)
        c.target_t[:, at(i * 128, 128, 128)] = target.T.astype(BF16)

    loop(c.high // 128, step)


def forward(c):
    chunks = c.hid_width // CHUNK

    def step(i):
        rows = at((i // chunks) * c.tile, c.tile, 128)
        cols = at((i % chunks) * CHUNK, CHUNK, CHUNK)
        k_rows = c.k[at(WINDOW + (i // chunks) * c.tile, c.tile, 128), :]
        gate = mm(k_rows, c.wg[:, cols])
        up = mm(k_rows, c.wu[:, cols])
        sig = logistic(gate)
        act = gate * sig
        c.hid[rows, cols] = (act * up).astype(BF16)
        c.act[rows, cols] = act
        c.slope[rows, cols] = up * (sig + act * (1.0 - sig))

    loop((c.high // c.tile) * chunks, step)


def backward(c):
    chunks = c.hid_width // CHUNK

    def step(i):
        rows = at((i // chunks) * c.tile, c.tile, 128)
        cols = at((i % chunks) * CHUNK, CHUNK, CHUNK)
        back = mm(c.target[rows, :], c.wdt[:, cols])
        c.d_gate[rows, cols] = (back * c.slope[rows, cols]).astype(BF16)
        c.d_up[rows, cols] = (back * c.act[rows, cols]).astype(BF16)

    loop((c.high // c.tile) * chunks, step)


def gradients(c):
    def step(i):
        cols = at(i * CHUNK, CHUNK, CHUNK)
        c.grad[0, :, cols] = mm(c.k_t[...], c.d_gate[:, cols])
        c.grad[1, :, cols] = mm(c.k_t[...], c.d_up[:, cols])
        c.grad[2, :, cols] = mm(c.target_t[...], c.hid[:, cols])

    loop(c.hid_width // CHUNK, step)

    def scale(m):
        grad = c.grad[m]
        frob = lax.rsqrt(jnp.sum(grad * grad, keepdims=True) + norm_epsilon)
        c.x[0, m] = (grad * frob).astype(BF16)

    loop(3, scale)


def newton(c):
    def sweep(turn):
        old, new = turn % 2, (turn + 1) % 2
        for m in range(3):
            x = c.x[old, m]
            c.a[m] = mm(x, x, 1, 1).astype(BF16)
        for m in range(3):
            a = c.a[m]
            c.p[m] = (cubic_coef * a.astype(F32) + quintic_coef * mm(a, a)).astype(BF16)
        for m in range(3):
            x = c.x[old, m]
            c.x[new, m] = (linear_coef * x.astype(F32) + mm(c.p[m], x)).astype(BF16)

    loop(NS_ITERS, sweep)


def renorm(c):
    def by_column(i):
        cols = at(i * CHUNK, CHUNK, CHUNK)
        for m, ref in ((0, c.wg), (1, c.wu)):
            w = ref[:, cols].astype(F32)
            u = w + c.x[NS_ITERS % 2, m, :, cols].astype(F32)
            want = jnp.sqrt(jnp.sum(w * w, axis=0, keepdims=True) + norm_epsilon)
            have = jnp.sqrt(jnp.sum(u * u, axis=0, keepdims=True) + norm_epsilon)
            c.x[NS_ITERS % 2, m, :, cols] = (u * (want / have)).astype(BF16)

    loop(c.hid_width // CHUNK, by_column)

    def by_row(i):
        rows = at(i * 128, 128, 128)
        w = c.wdt[rows, :].astype(F32)
        u = w + c.x[NS_ITERS % 2, 2, rows, :].astype(F32)
        want = jnp.sqrt(jnp.sum(w * w, axis=1, keepdims=True) + norm_epsilon)
        have = jnp.sqrt(jnp.sum(u * u, axis=1, keepdims=True) + norm_epsilon)
        c.x[NS_ITERS % 2, 2, rows, :] = (u * (want / have)).astype(BF16)

    loop(c.width // 128, by_row)


def attention(c, first, count):
    tile = WINDOW // 2
    power = math.log2(math.e) / math.sqrt(AHD)

    def step(i):
        t = first + i
        rows = at(t * tile, tile, tile)
        span = at(t * tile, WINDOW + tile, tile)
        below = lax.broadcasted_iota(jnp.int32, (tile, tile), 1) <= lax.broadcasted_iota(
            jnp.int32, (tile, tile), 0
        )
        far_bias = jnp.where(c.first_segment * (2 - t) > 0, F32(-1e30), F32(0.0))
        mid_bias = jnp.where(c.first_segment * (1 - t) > 0, F32(-1e30), F32(0.0))
        for head in range(c.width // AHD):
            feats = slice(head * AHD, (head + 1) * AHD)
            scores = mm(c.q[rows, feats], c.k[span, feats], 1, 1)
            edge = jnp.where(below, scores[:, 2 * tile :], scores[:, :tile] + far_bias)
            mid = scores[:, tile : 2 * tile] + mid_bias
            top = jnp.max(jnp.maximum(edge, mid), axis=1, keepdims=True)
            edge = jnp.exp2((edge - top) * power)
            mid = jnp.exp2((mid - top) * power)
            total = jnp.sum(edge + mid, axis=1, keepdims=True)
            weights = jnp.concatenate(
                [
                    jnp.where(below, 0.0, edge).astype(BF16),
                    mid.astype(BF16),
                    jnp.where(below, edge, 0.0).astype(BF16),
                ],
                axis=1,
            )
            mixed = mm(weights, c.v[span, feats])
            c.out[rows, feats] = (mixed / total).astype(BF16)

    loop(count, step)


def swiglu(c, start, gate, up, down, down_dim):
    q_rows = c.q[at(start, c.rows, c.rows), :]

    def step(i):
        cols = at(i * CHUNK, CHUNK, CHUNK)
        pre_gate = mm(q_rows, gate[:, cols])
        pre_up = mm(q_rows, up[:, cols])
        c.apply_hid[:, cols] = (pre_gate * logistic(pre_gate) * pre_up).astype(BF16)

    loop(c.hid_width // CHUNK, step)
    return mm(c.apply_hid[...], down[...], 1, down_dim)


def fast_rows(c, start):
    new = c.x.at[NS_ITERS % 2]

    @pl.when(start < c.high)
    def _():
        c.raw[...] = swiglu(c, start, c.wg, c.wu, c.wd, 0)

    @pl.when(start + c.rows > c.low)
    def _():
        after = swiglu(c, start, new.at[0], new.at[1], new.at[2], 1)
        place = start + lax.broadcasted_iota(jnp.int32, after.shape, 0)
        kept = (place < c.bound) & (place < c.high)
        c.raw[...] = jnp.where(kept, c.raw[...], after)

    raw = c.raw[...]
    rows = at(start, c.rows, c.rows)
    scale = lax.rsqrt(jnp.mean(raw * raw, axis=1, keepdims=True) + rms_epsilon)
    fast = (raw * scale * c.gain).astype(BF16)
    c.out[rows, :] = (c.out[rows, :].astype(F32) + fast.astype(F32)).astype(BF16)


def scratch_of(length, width, hid_width, rows, peers):
    low, high = length // 2 - length // 16, length // 2 + length // 16
    dma = pltpu.SemaphoreType.DMA
    return {
        "q": pltpu.VMEM((length, width), BF16),
        "k": pltpu.VMEM((WINDOW + length, width), BF16),
        "v": pltpu.VMEM((WINDOW + length, width), BF16),
        "rates": pltpu.VMEM((peers, 8, rows), F32),
        "out": pltpu.VMEM((length, width), BF16),
        "send": dma((4, peers)),
        "recv": dma((4, peers)),
        "own_sem": dma((4,)),
        "halo_send": dma((2,)),
        "halo_recv": dma((2,)),
        "out_send": dma((peers,)),
        "out_recv": dma((peers,)),
        "out_own": dma,
        "wg": pltpu.VMEM((width, hid_width), BF16),
        "wu": pltpu.VMEM((width, hid_width), BF16),
        "wd": pltpu.VMEM((hid_width, width), BF16),
        "wdt": pltpu.VMEM((width, hid_width), BF16),
        "target": pltpu.VMEM((high, width), BF16),
        "target_t": pltpu.VMEM((width, high), BF16),
        "k_t": pltpu.VMEM((width, high), BF16),
        "hid": pltpu.VMEM((high, hid_width), BF16),
        "d_gate": pltpu.VMEM((high, hid_width), BF16),
        "d_up": pltpu.VMEM((high, hid_width), BF16),
        "grad": pltpu.VMEM((3, width, hid_width), F32),
        "x": pltpu.VMEM((2, 3, width, hid_width), BF16),
        "act": pltpu.VMEM((high, hid_width), F32),
        "slope": pltpu.VMEM((high, hid_width), F32),
        "a": pltpu.VMEM((3, width, width), BF16),
        "p": pltpu.VMEM((3, width, width), BF16),
        "apply_hid": pltpu.VMEM((rows, hid_width), BF16),
        "raw": pltpu.VMEM((rows, width), F32),
        "w_sem": dma((3,)),
    }


def sizes(length, width, hid_width, rows):
    low, high = length // 2 - length // 16, length // 2 + length // 16
    return dict(
        length=length, width=width, hid_width=hid_width, rows=rows, low=low, high=high, tile=high // 3
    )


def flip(index, distance, count):
    result, place = 0, 1
    while place < count:
        bit = (index // place) % 2
        result = result + place * (1 - bit if distance & place else bit)
        place *= 2
    return result


def distances(peers):
    return sorted(range(1, peers), key=lambda d: (d > 1, d % 2, d))


def order_of(step, peers):
    half = peers // 2
    return jnp.where(
        step < half - 1, 2 * step + 2, jnp.where(step < peers - 2, 2 * (step - half) + 5, peers - 1 - step)
    )


def flip_by(index, distance, count):
    result, place = 0, 1
    while place < count:
        bit, other = (index // place) % 2, (distance // place) % 2
        result = result + place * (bit + other - 2 * bit * other)
        place *= 2
    return result


def place_of(peer, tok, group):
    return (tok - tok % 2 + peer // group, peer % group)


def feature_of(peer, group):
    return 2 * (peer % group) + peer // group


def greet(others):
    barrier = pltpu.get_barrier_semaphore()
    for other in others:
        pl.semaphore_signal(barrier, inc=1, device_id=other, device_id_type=MESH)
    pl.semaphore_wait(barrier, len(others))


def kernel(
    names, dims, group, toks, bounds, gain, q, k, v, r, gate_all, up_all, down_all, out, *scratch
):
    c = SimpleNamespace(**dims, **dict(zip(names, scratch)))
    tok, column = lax.axis_index("tok"), lax.axis_index("head")
    parity = tok % 2
    peers, rows, width = 2 * group, c.rows, c.width
    me = parity * group + column
    after = ((tok + 2) % toks, column)
    before = ((tok + toks - 2) % toks, column)
    weights = [
        pltpu.make_async_copy(whole.at[parity], mine, c.w_sem.at[i])
        for i, (whole, mine) in enumerate(((gate_all, c.wg), (up_all, c.wu), (down_all, c.wd)))
    ]
    for copy in weights:
        copy.start()
    c.gain = gain[2 * column + parity]
    c.bound = bounds[tok // 2]
    c.first_segment = jnp.where(tok < 2, 1, 0)
    greet([place_of(flip(me, d, peers), tok, group) for d in range(1, peers)] + [after, before])

    def source(t, peer):
        j = feature_of(peer, group)
        if t == 3:
            return r.at[j]
        return (k, v, q)[t].at[:, at(j * width, width, width)]

    def slot(t, peer):
        if t == 3:
            return c.rates.at[peer]
        shift = WINDOW if t < 2 else 0
        return (c.k, c.v, c.q)[t].at[at(shift + peer * rows, rows, rows), :]

    def remote(t, peer):
        return pltpu.make_async_remote_copy(
            source(t, peer), slot(t, me), c.send.at[t, peer], c.recv.at[t, me],
            device_id=place_of(peer, tok, group), device_id_type=MESH,
        )

    def own(t):
        return pltpu.make_async_copy(source(t, me), slot(t, me), c.own_sem.at[t])

    def arrived(t, peer):
        @pl.when(me != peer)
        def _():
            pltpu.make_async_remote_copy(
                slot(t, peer), slot(t, peer), c.send.at[t, peer], c.recv.at[t, peer],
                device_id=place_of(peer, tok, group), device_id_type=MESH,
            ).wait_recv()

        @pl.when(me == peer)
        def _():
            own(t).wait()

    def block(peer):
        return out.at[:, at(feature_of(peer, group) * width, width, width)]

    def done_rows(peer):
        return c.out.at[at(peer * rows, rows, rows), :]

    def give(peer):
        return pltpu.make_async_remote_copy(
            done_rows(peer), block(me), c.out_send.at[peer], c.out_recv.at[me],
            device_id=place_of(peer, tok, group), device_id_type=MESH,
        )

    def taken(peer):
        return pltpu.make_async_remote_copy(
            done_rows(peer), block(peer), c.out_send.at[peer], c.out_recv.at[peer],
            device_id=place_of(peer, tok, group), device_id_type=MESH,
        )

    order = distances(peers)
    for t in (3, 0):
        for d in order:
            remote(t, flip(me, d, peers)).start()
        own(t).start()

    halos = [
        pltpu.make_async_remote_copy(
            o.at[pl.ds(c.length, WINDOW), :], o.at[pl.ds(0, WINDOW), :],
            c.halo_send.at[t], c.halo_recv.at[t], device_id=after, device_id_type=MESH,
        )
        for t, o in enumerate((c.k, c.v))
    ]

    def send_next(t):
        for d in order:
            remote(t - 1, flip(me, d, peers)).wait_send()
            remote(t, flip(me, d, peers)).start()
        own(t).start()

    for copy in weights:
        copy.wait()
    transpose_down(c)
    send_next(1)
    needed = -(-c.high // rows)
    for p in range(needed):
        arrived(0, p)
    for p in range(needed, peers):
        arrived(0, p)
    halos[0].start()
    forward(c)
    transpose_keys(c)
    send_next(2)
    for p in range(peers):
        arrived(3, p)
    for p in range(needed):
        arrived(1, p)
    for p in range(needed, peers):
        arrived(1, p)
    halos[1].start()
    make_targets(c)
    backward(c)
    gradients(c)
    newton(c)
    renorm(c)
    for halo in halos:
        halo.wait()
    tiles = rows // (WINDOW // 2)

    def turn(step):
        peer = flip_by(me, jnp.where(step == 0, 0, order_of(step - 1, peers)), peers)
        arrived(2, peer)
        attention(c, peer * tiles, tiles)
        fast_rows(c, peer * rows)

        @pl.when(peer != me)
        def _():
            give(peer).start()

        @pl.when(peer == me)
        def _():
            pltpu.make_async_copy(done_rows(me), block(me), c.out_own).start()

    loop(peers, turn)
    pltpu.make_async_copy(done_rows(me), block(me), c.out_own).wait()
    for d in order:
        taken(flip(me, d, peers)).wait_recv()
    for d in order:
        give(flip(me, d, peers)).wait_send()
        for t in (2, 3):
            remote(t, flip(me, d, peers)).wait_send()


def body(queries, keys, values, token_rates, gate_start, up_start, down_start, norm_gain, bounds):
    rows, feats = queries.shape
    group, toks = lax.axis_size("head"), lax.axis_size("tok")
    heads, width, hid_width = token_rates.shape[1], gate_start.shape[1], gate_start.shape[2]
    peers = 2 * group
    length = peers * rows
    anywhere = pl.BlockSpec(memory_space=pl.ANY)
    vmem = pl.BlockSpec(memory_space=pltpu.VMEM)
    dma = pltpu.SemaphoreType.DMA
    rates = jnp.broadcast_to(token_rates.T.astype(F32)[:, None, :], (heads, 8, rows))
    scratch = scratch_of(length, width, hid_width, rows, peers)
    return pl.pallas_call(
        functools.partial(
            kernel, tuple(scratch), sizes(length, width, hid_width, rows), group, toks
        ),
        out_shape=jax.ShapeDtypeStruct((rows, feats), BF16),
        in_specs=[pl.BlockSpec(memory_space=pltpu.SMEM), vmem] + [anywhere] * 7,
        out_specs=anywhere,
        scratch_shapes=list(scratch.values()),
        compiler_params=pltpu.CompilerParams(
            collective_id=0, has_side_effects=True, vmem_limit_bytes=66000000
        ),
        name="layer",
    )(
        bounds, norm_gain.reshape(heads, 1, width), queries, keys, values, rates,
        gate_start, up_start, down_start,
    )


def solution(mesh):
    spread = P(("tok", "head"), None)
    owned = P("head", None, None)
    return jax.shard_map(
        body,
        mesh=mesh,
        in_specs=(spread,) * 4 + (owned,) * 3 + (P(), P()),
        out_specs=spread,
        check_vma=False,
    )
```
